32 devices in a mesh: img: 8 (over z, y), seq: 4 (over x, core).
Axes of the slice: x: 2, y: 2, z: 4, core: 2. Of those that a mesh axis runs over, the one named last changes fastest.
Arguments:
- tokens: bfloat16 [8, 512, 1152], P('img', 'seq'), may hold values from -6 to 6
- counts: int32 [8, 4], P('img'), may hold values from 96 to 128, as said below
- w_qkv: bfloat16 [3981312], P(('img', 'seq')), may hold values from -1 to 1
- w_out: bfloat16 [1327104], P(('img', 'seq')), may hold values from -1.5 to 1.5
- w_fc1: bfloat16 [4958208], P(('img', 'seq')), may hold values from -0.1875 to 0.1875
- w_fc2: bfloat16 [4958208], P(('img', 'seq')), may hold values from -0.09375 to 0.09375
- vectors: bfloat16 [13536], P(('img', 'seq')), may hold values from -2 to 2
- cotangent: bfloat16 [8, 512, 1152], P('img', 'seq'), may hold values from -6 to 6
Outputs:
- output: bfloat16 [8, 512, 1152], P('img', 'seq')
- input_grad: float32 [8, 512, 1152], P('img', 'seq')
- grad_qkv: float32 [3981312], P(('img', 'seq'))
- grad_out: float32 [1327104], P(('img', 'seq'))
- grad_fc1: float32 [4958208], P(('img', 'seq'))
- grad_fc2: float32 [4958208], P(('img', 'seq'))
- grad_vectors: float32 [11232], P(('img', 'seq'))
- grad_front: float32 [2304], P(('img', 'seq'))
The draws below stay inside these ranges and needn't reach their ends.
Inputs may be any that keep to these rules, and one draw needn't show every extreme that they name: An image's counts come from one length L of 385 to 512 tokens: every slice gets L // 4 and the first L mod 4 slices one more; some image is full in every draw.
All inputs are finite; a program needn't handle non-finite values.
Results may differ from the reference program's by a relative error of at most 0.011.
Values may be sent and summed in bfloat16 or wider, within the bound.
A program may use at most 320 MiB of HBM per device.

```python
import jax
import jax.numpy as jnp
from jax import lax

D = 1152
HEADS = 16
HEAD_DIM = 72
FF = 4304
SLOT = 128
IMAGES = 8
VECS = 13536
N_SEQ = 4


def draw_counts(key, part):
    key_len = jax.random.fold_in(key, 11)
    key_full = jax.random.fold_in(key, 12)
    lengths = jax.random.randint(key_len, (IMAGES,), 3 * SLOT + 1, 4 * SLOT + 1)
    full_image = jax.random.randint(key_full, (), 0, IMAGES)
    lengths = jnp.where(jnp.arange(IMAGES) == full_image, 4 * SLOT, lengths)
    base = lengths // N_SEQ
    extra = lengths % N_SEQ
    result = base[:, None] + (jnp.arange(N_SEQ)[None, :] < extra[:, None]).astype(jnp.int32)
    return result.astype(jnp.int32)


def draw_w_qkv(key, part):
    key_base = jax.random.fold_in(key, 21)
    base = jnp.clip(jax.random.normal(key_base, (D, 3 * D), jnp.float32), -6.0, 6.0) / jnp.sqrt(jnp.float32(D))
    whole = base
    return jnp.clip(whole, -1.0, 1.0).reshape(-1).astype(jnp.bfloat16)


def draw_vectors(key, part):
    key_vals = jax.random.fold_in(key, 31)
    position = jnp.arange(VECS)
    block = position // D
    is_gain = (block == 2) | (block == 5)
    raw = jax.random.normal(key_vals, (VECS,), jnp.float32)
    values = jnp.where(is_gain, 1.0 + 0.1 * jnp.clip(raw, -3.0, 3.0), 0.5 * jnp.clip(raw, -4.0, 4.0))
    return values.astype(jnp.bfloat16)


def steps_of(stream_key, dims, cuts, least, largest):
    def one(dim, blocks):
        draws = jax.random.uniform(jax.random.fold_in(jax.random.fold_in(stream_key, 6), dim), (blocks,), jnp.float32, least / len(cuts), largest / len(cuts))
        return jnp.repeat(jnp.exp(draws), dims[dim] // blocks).reshape((-1,) + (1,) * (len(dims) - dim - 1))

    factor_of = one(*cuts[0])
    for cut in cuts[1:]:
        factor_of = factor_of * one(*cut)
    return factor_of


def noise(stream_key, extent, width, most, split=(), held_as=jnp.bfloat16):
    entries = width * jax.random.normal(stream_key, extent, jnp.float32)
    if split:
        entries = entries * steps_of(stream_key, extent, split, -0.22, 0.18)
    return jnp.clip(entries, -most, most).astype(held_as)


def setup_inputs(seed: int = 0) -> dict:
    streams_of = jax.random.split(jax.random.key(seed), 9)
    return {
        "tokens": noise(streams_of[0], (IMAGES, N_SEQ * SLOT, D), 1.0, 6.0, ((0, 8), (1, 4))),
        "counts": draw_counts(jax.random.fold_in(streams_of[8], 71), 0),
        "w_qkv": draw_w_qkv(jax.random.fold_in(streams_of[8], 71), 0),
        "w_out": noise(streams_of[3], (D * D,), (max(D * 8 // (N_SEQ * SLOT), 1)) ** -0.5, 1.5, ((0, 32),)),
        "w_fc1": noise(streams_of[4], (D * FF,), D ** -0.5, 0.1875, ((0, 32),)),
        "w_fc2": noise(streams_of[5], (FF * D,), FF ** -0.5, 0.09375, ((0, 32),)),
        "vectors": draw_vectors(jax.random.fold_in(streams_of[8], 71), 0),
        "cotangent": noise(streams_of[7], (IMAGES, N_SEQ * SLOT, D), 1.0, 6.0, ((0, 8), (1, 4))),
    }


EPS = 1e-06
GELU_C = 0.7978845608028654

def normalize(values):
    mean = lax.optimization_barrier(jnp.mean(values, axis=-1, keepdims=True))
    centred = values - mean
    rstd = lax.rsqrt(lax.optimization_barrier(jnp.mean(centred * centred, axis=-1, keepdims=True)) + EPS)
    return (centred * rstd, rstd)

def norm_back(grad_in, normed, rstd, gain):
    scaled = grad_in * gain
    return rstd * (scaled - lax.optimization_barrier(jnp.mean(scaled, axis=-1, keepdims=True)) - normed * lax.optimization_barrier(jnp.mean(scaled * normed, axis=-1, keepdims=True)))

def gelu_parts(pre):
    inner = GELU_C * (pre + 0.044715 * pre * pre * pre)
    tanh_v = jnp.tanh(inner)
    value = 0.5 * pre * (1.0 + tanh_v)
    slope = 0.5 * (1.0 + tanh_v) + 0.5 * pre * (1.0 - tanh_v * tanh_v) * GELU_C * (1.0 + 3.0 * 0.044715 * pre * pre)
    return (value, slope)

def split_heads(values):
    return values.astype(jnp.float32).reshape(values.shape[0], HEADS, HEAD_DIM)

def masked_scores(queries, keys, key_valid):
    scale = HEAD_DIM ** (-0.5)
    scores = jnp.einsum('shd,thd->hst', split_heads(queries), split_heads(keys)) * scale
    return jnp.where(key_valid[None, None, :], scores, -1e+30)

def reference(tokens, counts, w_qkv, w_out, w_fc1, w_fc2, vectors, cotangent):
    f32 = jnp.float32
    bf16 = jnp.bfloat16
    mat_qkv = w_qkv.reshape(D, 3 * D)
    mat_out = w_out.reshape(D, D)
    mat_fc1 = w_fc1.reshape(D, FF)
    mat_fc2 = w_fc2.reshape(FF, D)
    vec = vectors.astype(f32)
    bias1, v_bias, gain1, q_bias, out_bias, gain2, bias2, fc2_bias = [vec[i * D:(i + 1) * D] for i in range(8)]
    fc1_bias = vec[8 * D:8 * D + FF]
    scale = HEAD_DIM ** (-0.5)

    def one_image(carry, item):
        acc_qkv, acc_out, acc_fc1, acc_fc2, acc_vec = carry
        x_img, cnt, cot = item
        valid = (jnp.arange(SLOT)[None, :] < cnt[:, None]).reshape(-1)
        rowmask = valid.astype(f32)[:, None]
        x = x_img.astype(f32)
        normed1, rstd1 = normalize(x)
        ln1 = (normed1 * gain1 + bias1).astype(bf16)
        qkv = jnp.dot(ln1, mat_qkv, preferred_element_type=f32)
        queries = (qkv[:, :D] + q_bias).astype(bf16)
        keys = qkv[:, D:2 * D].astype(bf16)
        values = (qkv[:, 2 * D:] + v_bias).astype(bf16)
        scores = masked_scores(queries, keys, valid)
        top = lax.optimization_barrier(jnp.max(scores, axis=-1, keepdims=True))
        lse = top + jnp.log(lax.optimization_barrier(jnp.sum(jnp.exp(scores - top), axis=-1, keepdims=True)))
        probs = jnp.exp(scores - lse).astype(bf16)
        mixed = jnp.einsum('hst,thd->shd', probs.astype(f32), split_heads(values)).reshape(-1, D).astype(bf16)
        resid = x + jnp.dot(mixed, mat_out, preferred_element_type=f32) + out_bias
        normed2, rstd2 = normalize(resid)
        ln2 = (normed2 * gain2 + bias2).astype(bf16)
        pre = jnp.dot(ln2, mat_fc1, preferred_element_type=f32) + fc1_bias
        act_f, slope = gelu_parts(pre)
        act = act_f.astype(bf16)
        out_img = ((resid + jnp.dot(act, mat_fc2, preferred_element_type=f32) + fc2_bias) * rowmask).astype(bf16)
        grad_y = cot.astype(f32) * rowmask
        grad_y16 = grad_y.astype(bf16)
        g_fc2 = jnp.dot(act.T, grad_y16, preferred_element_type=f32)
        grad_act = jnp.dot(grad_y16, mat_fc2.T, preferred_element_type=f32)
        grad_pre = grad_act * slope
        grad_pre16 = grad_pre.astype(bf16)
        g_fc1 = jnp.dot(ln2.T, grad_pre16, preferred_element_type=f32)
        grad_ln2 = jnp.dot(grad_pre16, mat_fc1.T, preferred_element_type=f32)
        grad_resid = grad_y + norm_back(grad_ln2, normed2, rstd2, gain2)
        grad_resid16 = grad_resid.astype(bf16)
        g_out = jnp.dot(mixed.T, grad_resid16, preferred_element_type=f32)
        grad_mixed16 = jnp.dot(grad_resid16, mat_out.T, preferred_element_type=f32).astype(bf16)
        gm_heads = split_heads(grad_mixed16)
        delta = jnp.einsum('shd,shd->hs', gm_heads, split_heads(mixed))
        grad_values = jnp.einsum('hst,shd->thd', probs.astype(f32), gm_heads).reshape(-1, D)
        dots = jnp.einsum('shd,thd->hst', gm_heads, split_heads(values))
        grad_scores = (jnp.exp(scores - lse) * (dots - delta[:, :, None]) * scale).astype(bf16)
        grad_queries = jnp.einsum('hst,thd->shd', grad_scores.astype(f32), split_heads(keys)).reshape(-1, D)
        grad_keys = jnp.einsum('hst,shd->thd', grad_scores.astype(f32), split_heads(queries)).reshape(-1, D)
        grad_qkv16 = jnp.concatenate([grad_queries.astype(bf16), grad_keys.astype(bf16), grad_values.astype(bf16)], axis=1)
        g_qkv = jnp.dot(ln1.T, grad_qkv16, preferred_element_type=f32)
        grad_ln1 = jnp.dot(grad_qkv16, mat_qkv.T, preferred_element_type=f32)
        grad_in = grad_resid + norm_back(grad_ln1, normed1, rstd1, gain1)
        g_vec = jnp.concatenate([lax.optimization_barrier(jnp.sum(grad_ln1, axis=0)), lax.optimization_barrier(jnp.sum(grad_values, axis=0)), lax.optimization_barrier(jnp.sum(grad_ln1 * normed1, axis=0)), lax.optimization_barrier(jnp.sum(grad_queries, axis=0)), lax.optimization_barrier(jnp.sum(grad_resid, axis=0)), lax.optimization_barrier(jnp.sum(grad_ln2 * normed2, axis=0)), lax.optimization_barrier(jnp.sum(grad_ln2, axis=0)), lax.optimization_barrier(jnp.sum(grad_y, axis=0)), lax.optimization_barrier(jnp.sum(grad_pre, axis=0))])
        carry = (acc_qkv + g_qkv, acc_out + g_out, acc_fc1 + g_fc1, acc_fc2 + g_fc2, acc_vec + g_vec)
        return (carry, (out_img, grad_in))
    init = (jnp.zeros((D, 3 * D), f32), jnp.zeros((D, D), f32), jnp.zeros((D, FF), f32), jnp.zeros((FF, D), f32), jnp.zeros((8 * D + FF,), f32))
    carry, (outputs, input_grads) = lax.scan(one_image, init, (tokens, counts, cotangent))
    acc_qkv, acc_out, acc_fc1, acc_fc2, acc_vec = carry
    grad_front = acc_vec[:2 * D]
    grad_vectors = jnp.concatenate([acc_vec[2 * D:], jnp.zeros((VECS - 8 * D - FF,), f32)])
    return (outputs, input_grads, acc_qkv.reshape(-1), acc_out.reshape(-1), acc_fc1.reshape(-1), acc_fc2.reshape(-1), grad_vectors, grad_front)
```

```python
import jax
import jax.numpy as jnp
from jax import lax
from jax.sharding import PartitionSpec as P

HEADS = 16
HEAD_DIM = 72


EPS = 1e-06
GELU_C = 0.7978845608028654


def normalize(values):
    mean = jnp.mean(values, axis=-1, keepdims=True)
    centred = values - mean
    rstd = lax.rsqrt(jnp.mean(centred * centred, axis=-1, keepdims=True) + EPS)
    return (centred * rstd, rstd)


def norm_back(grad_in, normed, rstd, gain):
    scaled = grad_in * gain
    return rstd * (
        scaled
        - jnp.mean(scaled, axis=-1, keepdims=True)
        - normed * jnp.mean(scaled * normed, axis=-1, keepdims=True)
    )


def gelu_parts(pre):
    inner = GELU_C * (pre + 0.044715 * pre * pre * pre)
    tanh_v = jnp.tanh(inner)
    value = 0.5 * pre * (1.0 + tanh_v)
    slope = 0.5 * (1.0 + tanh_v) + 0.5 * pre * (1.0 - tanh_v * tanh_v) * GELU_C * (
        1.0 + 3.0 * 0.044715 * pre * pre
    )
    return (value, slope)


TILE = 2048
LANES = 128


def round_up(value, step):
    return -(-value // step) * step


def pack(flat):
    padded = round_up(flat.shape[0], TILE)
    return jnp.pad(flat, (0, padded - flat.shape[0])).reshape(-1, LANES)


def unpack_blocks(packed, blocks, length):
    return packed.reshape(blocks, -1)[:, :length].reshape(-1)


def pack_blocks(flat, blocks):
    block = flat.reshape(blocks, -1)
    padded = round_up(block.shape[1], TILE)
    return jnp.pad(block, ((0, 0), (0, padded - block.shape[1]))).reshape(-1, LANES)


def gather(value, axes):
    return lax.all_gather(value, axes, axis=0, tiled=True)


def scatter_sum(value, axes):
    return lax.psum_scatter(value, axes, scatter_dimension=0, tiled=True)


def weight_grad(left, right):
    return lax.dot_general(
        left, right, (((0,), (0,)), ((), ())), preferred_element_type=jnp.float32
    ).astype(jnp.bfloat16)


def dot_t(left, right):
    return lax.dot_general(
        left, right, (((1,), (1,)), ((), ())), preferred_element_type=jnp.float32
    )


def batched(left, right, over_left, over_right):
    return lax.dot_general(
        left,
        right,
        (((over_left,), (over_right,)), ((0,), (0,))),
        preferred_element_type=jnp.float32,
    )


def shards(tokens, counts, w_qkv, w_out, w_fc1, w_fc2, vectors, cotangent):
    f32 = jnp.float32
    bf16 = jnp.bfloat16
    width = tokens.shape[2]
    slot = tokens.shape[1]
    scale = HEAD_DIM ** (-0.5)
    position = lax.axis_index("seq")
    seq_count = lax.axis_size("seq")
    img_count = lax.axis_size("img")
    device_count = img_count * seq_count
    both = ("img", "seq")
    shard_qkv, shard_out, shard_fc1, shard_fc2, shard_vec = (
        w.shape[0] for w in (w_qkv, w_out, w_fc1, w_fc2, vectors)
    )
    hidden = shard_fc1 * device_count // width
    heads = HEADS // seq_count
    cols = width // seq_count
    units = hidden // seq_count
    rows = width // img_count
    pad_cols = round_up(3 * cols, LANES) - 3 * cols
    pad_units = round_up(units, LANES) - units
    to_quarter = [(c, (c % img_count) * seq_count + c // img_count) for c in range(device_count)]
    to_owner = [(b, a) for a, b in to_quarter]

    slice_counts = counts[0]
    key_valid = (jnp.arange(slot)[None, :] < slice_counts[:, None]).reshape(-1)
    row_valid = lax.dynamic_slice_in_dim(key_valid, position * slot, slot)
    rowmask = row_valid.astype(f32)[:, None]

    def mine(values):
        return lax.dynamic_slice_in_dim(values, position * slot, slot)

    qkv_seq = unpack_blocks(gather(pack(w_qkv), "seq"), seq_count, shard_qkv)
    out_vec = gather(pack(jnp.concatenate([w_out, vectors])), both)
    x_all16 = gather(tokens[0], "seq")
    qkv_rows = qkv_seq.reshape(rows, 3 * width)
    qkv_part = jnp.concatenate(
        [
            lax.dynamic_slice_in_dim(qkv_rows, j * width + position * cols, cols, axis=1)
            for j in range(3)
        ]
        + [jnp.zeros((rows, pad_cols), bf16)],
        axis=1,
    )
    mat_qkv = gather(qkv_part, "img")
    fc1_seq = unpack_blocks(gather(pack(w_fc1), "seq"), seq_count, shard_fc1)
    fc1_part = jnp.pad(
        lax.dynamic_slice_in_dim(
            fc1_seq.reshape(rows, hidden), position * units, units, axis=1
        ),
        ((0, 0), (0, pad_units)),
    )
    mat_fc1 = gather(fc1_part, "img")
    fc2_chunk = lax.ppermute(pack(w_fc2), both, to_quarter)
    mat_fc2 = jnp.pad(
        unpack_blocks(gather(fc2_chunk, "img"), img_count, shard_fc2).reshape(units, width),
        ((0, pad_units), (0, 0)),
    )
    cot_all = gather(cotangent[0], "seq")

    blocks_ov = out_vec.reshape(device_count, -1)
    mat_out = blocks_ov[:, :shard_out].reshape(width, width)
    vec = blocks_ov[:, shard_out : shard_out + shard_vec].reshape(-1).astype(f32)
    bias1, v_bias, gain1, q_bias, out_bias, gain2, bias2, fc2_bias = (
        vec[i * width : (i + 1) * width] for i in range(8)
    )
    fc1_bias = vec[8 * width : 8 * width + hidden]

    def my_cols(values):
        return lax.dynamic_slice_in_dim(values, position * cols, cols)

    fc1_bias_mine = jnp.pad(
        lax.dynamic_slice_in_dim(fc1_bias, position * units, units), (0, pad_units)
    )

    x = x_all16.astype(f32)
    normed1, _ = normalize(x)
    ln1 = (normed1 * gain1 + bias1).astype(bf16)
    qkv = jnp.dot(ln1, mat_qkv, preferred_element_type=f32)

    def by_head(values):
        return values.reshape(-1, heads, HEAD_DIM).transpose(1, 0, 2)

    def by_slot(values):
        return values.transpose(1, 0, 2).reshape(-1, cols)

    queries = by_head((qkv[:, :cols] + my_cols(q_bias)).astype(bf16))
    keys = by_head(qkv[:, cols : 2 * cols].astype(bf16))
    values = by_head((qkv[:, 2 * cols : 3 * cols] + my_cols(v_bias)).astype(bf16))
    scores = batched(queries, keys, 2, 2) * scale
    scores = jnp.where(key_valid[None, None, :], scores, -1e30)
    top = jnp.max(scores, axis=-1, keepdims=True)
    lse = top + jnp.log(jnp.sum(jnp.exp(scores - top), axis=-1, keepdims=True))
    probs = jnp.exp(scores - lse).astype(bf16)
    mixed_heads = batched(probs, values, 2, 1)
    mixed_mine = by_slot(mixed_heads).astype(bf16)
    mixed = lax.all_gather(mixed_mine, "seq", axis=0, tiled=True)
    mixed = (
        mixed.reshape(seq_count, -1, cols).transpose(1, 0, 2).reshape(-1, width)
    )
    resid = x + jnp.dot(mixed, mat_out, preferred_element_type=f32) + out_bias
    normed2, rstd2 = normalize(resid)
    ln2 = (normed2 * gain2 + bias2).astype(bf16)
    pre = jnp.dot(ln2, mat_fc1, preferred_element_type=f32) + fc1_bias_mine
    act_f, slope = gelu_parts(pre)
    act = act_f.astype(bf16)

    grad_y16 = jnp.where(key_valid[:, None], cot_all, jnp.zeros((), bf16))
    grad_pre = dot_t(grad_y16, mat_fc2) * slope
    grad_pre16 = grad_pre.astype(bf16)
    grad_ln2 = scatter_sum(dot_t(grad_pre16, mat_fc1).astype(bf16), "seq").astype(f32)
    grad_y = cotangent[0].astype(f32) * rowmask
    normed2_mine = mine(normed2)
    grad_resid = grad_y + norm_back(grad_ln2, normed2_mine, mine(rstd2), gain2)
    grad_resid16 = gather(grad_resid.astype(bf16), "seq")

    def reduce_rows(partial):
        return scatter_sum(partial, "img")

    sum_fc1 = reduce_rows(weight_grad(ln2, grad_pre16))
    sum_fc2 = reduce_rows(
        pack_blocks(weight_grad(act, grad_y16)[:units].reshape(-1), img_count)
    )
    out_terms = scatter_sum(
        jnp.dot(act, mat_fc2, preferred_element_type=f32).astype(bf16), "seq"
    ).astype(f32)
    output = ((mine(resid) + out_terms + fc2_bias) * rowmask).astype(bf16)

    out_mine = lax.dynamic_slice_in_dim(mat_out, position * cols, cols)
    gm = by_head(dot_t(grad_resid16, out_mine).astype(bf16))
    mixed_back = by_head(mixed_mine)
    delta = jnp.sum(gm.astype(f32) * mixed_back.astype(f32), axis=-1, keepdims=True)
    grad_values = by_slot(batched(probs, gm, 1, 1))
    dots = batched(gm, values, 2, 2)
    grad_scores = (jnp.exp(scores - lse) * (dots - delta) * scale).astype(bf16)
    grad_queries = by_slot(batched(grad_scores, keys, 2, 1))
    grad_keys = by_slot(batched(grad_scores, queries, 1, 1))
    grad_qkv16 = jnp.concatenate(
        [grad_queries.astype(bf16), grad_keys.astype(bf16), grad_values.astype(bf16)]
        + [jnp.zeros((seq_count * slot, pad_cols), bf16)],
        axis=1,
    )
    grad_ln1 = scatter_sum(dot_t(grad_qkv16, mat_qkv).astype(bf16), "seq").astype(f32)
    sum_qkv = reduce_rows(weight_grad(ln1, grad_qkv16))
    sum_out = reduce_rows(
        pack_blocks(weight_grad(mixed_mine, grad_resid16).reshape(-1), img_count)
    )
    normed1_mine, rstd1_mine = normalize(tokens[0].astype(f32))
    input_grad = grad_resid + norm_back(grad_ln1, normed1_mine, rstd1_mine, gain1)

    def own_block(rows_sum, thirds, used, size):
        blocks = gather(rows_sum, "seq").reshape(seq_count, rows, -1)[:, :, : thirds * used]
        whole = blocks.reshape(seq_count, rows, thirds, used).transpose(1, 2, 0, 3)
        return lax.dynamic_slice_in_dim(whole.reshape(-1), position * size, size).astype(f32)

    def own_chunk(packed, size):
        return lax.ppermute(packed, both, to_owner).reshape(-1)[:size].astype(f32)

    grad_fc1 = own_block(sum_fc1, 1, units, shard_fc1)
    grad_fc2 = own_chunk(sum_fc2, shard_fc2)
    grad_qkv = own_block(sum_qkv, 3, cols, shard_qkv)
    grad_out = own_chunk(sum_out, shard_out)

    def spread(part, full):
        return lax.dynamic_update_slice_in_dim(
            jnp.zeros((full,), f32), part, position * part.shape[0], 0
        )

    shard_front = 2 * width // device_count
    unused = shard_vec * device_count - 8 * width - hidden
    g_front = jnp.concatenate(
        [jnp.sum(grad_ln1, axis=0), spread(jnp.sum(grad_values, axis=0), width)]
    )
    g_rest = jnp.concatenate(
        [
            jnp.sum(grad_ln1 * normed1_mine, axis=0),
            spread(jnp.sum(grad_queries, axis=0), width),
            jnp.sum(grad_resid, axis=0),
            jnp.sum(grad_ln2 * normed2_mine, axis=0),
            jnp.sum(grad_ln2, axis=0),
            jnp.sum(grad_y, axis=0),
            spread(jnp.sum(grad_pre, axis=0)[:units], hidden),
            jnp.zeros((unused,), f32),
        ]
    )
    g_vec = jnp.concatenate(
        [g_front.reshape(device_count, -1), g_rest.reshape(device_count, -1)], axis=1
    )
    g_vec = jnp.pad(g_vec, ((0, 0), (0, round_up(shard_vec, 1024) - shard_vec)))
    vec_mine = scatter_sum(g_vec.reshape(-1, LANES), both).reshape(-1)
    return (
        output[None],
        input_grad[None],
        grad_qkv,
        grad_out,
        grad_fc1,
        grad_fc2,
        vec_mine[shard_front:shard_vec],
        vec_mine[:shard_front],
    )


def solution(mesh):
    return jax.shard_map(
        shards,
        mesh=mesh,
        in_specs=(
            P("img", "seq", None),
            P("img", None),
            P(("img", "seq")),
            P(("img", "seq")),
            P(("img", "seq")),
            P(("img", "seq")),
            P(("img", "seq")),
            P("img", "seq", None),
        ),
        out_specs=(
            P("img", "seq", None),
            P("img", "seq", None),
            P(("img", "seq")),
            P(("img", "seq")),
            P(("img", "seq")),
            P(("img", "seq")),
            P(("img", "seq")),
            P(("img", "seq")),
        ),
        check_vma=False,
    )
```

```python
import jax
import jax.numpy as jnp
from jax import lax
from jax.sharding import PartitionSpec as P

HEADS = 16
HEAD_DIM = 72


EPS = 1e-06
GELU_C = 0.7978845608028654


def normalize(values):
    mean = jnp.mean(values, axis=-1, keepdims=True)
    centred = values - mean
    rstd = lax.rsqrt(jnp.mean(centred * centred, axis=-1, keepdims=True) + EPS)
    return (centred * rstd, rstd)


def norm_back(grad_in, normed, rstd, gain):
    scaled = grad_in * gain
    return rstd * (
        scaled
        - jnp.mean(scaled, axis=-1, keepdims=True)
        - normed * jnp.mean(scaled * normed, axis=-1, keepdims=True)
    )


def gelu_parts(pre):
    inner = GELU_C * (pre + 0.044715 * pre * pre * pre)
    tanh_v = jnp.tanh(inner)
    value = 0.5 * pre * (1.0 + tanh_v)
    slope = 0.5 * (1.0 + tanh_v) + 0.5 * pre * (1.0 - tanh_v * tanh_v) * GELU_C * (
        1.0 + 3.0 * 0.044715 * pre * pre
    )
    return (value, slope)


TILE = 2048
LANES = 128


def round_up(value, step):
    return -(-value // step) * step


def pack(flat):
    padded = round_up(flat.shape[0], TILE)
    return jnp.pad(flat, (0, padded - flat.shape[0])).reshape(-1, LANES)


def unpack_blocks(packed, blocks, length):
    return packed.reshape(blocks, -1)[:, :length].reshape(-1)


def pack_blocks(flat, blocks):
    block = flat.reshape(blocks, -1)
    padded = round_up(block.shape[1], TILE)
    return jnp.pad(block, ((0, 0), (0, padded - block.shape[1]))).reshape(-1, LANES)


def gather(value, axes):
    return lax.all_gather(value, axes, axis=0, tiled=True)


def scatter_sum(value, axes):
    return lax.psum_scatter(value, axes, scatter_dimension=0, tiled=True)


def weight_grad(left, right):
    return lax.dot_general(
        left, right, (((0,), (0,)), ((), ())), preferred_element_type=jnp.float32
    ).astype(jnp.bfloat16)


def dot_t(left, right):
    return lax.dot_general(
        left, right, (((1,), (1,)), ((), ())), preferred_element_type=jnp.float32
    )


def batched(left, right, over_left, over_right):
    return lax.dot_general(
        left,
        right,
        (((over_left,), (over_right,)), ((0,), (0,))),
        preferred_element_type=jnp.float32,
    )


def shards(tokens, counts, w_qkv, w_out, w_fc1, w_fc2, vectors, cotangent):
    f32 = jnp.float32
    bf16 = jnp.bfloat16
    width = tokens.shape[2]
    slot = tokens.shape[1]
    scale = HEAD_DIM ** (-0.5)
    position = lax.axis_index("seq")
    seq_count = lax.axis_size("seq")
    img_count = lax.axis_size("img")
    device_count = img_count * seq_count
    both = ("img", "seq")
    shard_qkv, shard_out, shard_fc1, shard_fc2, shard_vec = (
        w.shape[0] for w in (w_qkv, w_out, w_fc1, w_fc2, vectors)
    )
    hidden = shard_fc1 * device_count // width
    heads = HEADS // seq_count
    cols = width // seq_count
    units = hidden // seq_count
    rows = width // img_count
    pad_cols = round_up(3 * cols, LANES) - 3 * cols
    pad_units = round_up(units, LANES) - units
    to_quarter = [(c, (c % img_count) * seq_count + c // img_count) for c in range(device_count)]
    to_owner = [(b, a) for a, b in to_quarter]

    slice_counts = counts[0]
    key_valid = (jnp.arange(slot)[None, :] < slice_counts[:, None]).reshape(-1)
    row_valid = lax.dynamic_slice_in_dim(key_valid, position * slot, slot)
    rowmask = row_valid.astype(f32)[:, None]

    def mine(values):
        return lax.dynamic_slice_in_dim(values, position * slot, slot)

    shard_ov = shard_out + shard_vec
    local = gather(pack(jnp.concatenate([w_qkv, w_fc1, w_out, vectors])), "seq")
    local = local.reshape(seq_count, -1)
    x_all16 = gather(tokens[0], "seq")
    qkv_rows = local[:, :shard_qkv].reshape(rows, 3 * width)
    fc1_rows = local[:, shard_qkv : shard_qkv + shard_fc1].reshape(rows, hidden)
    ov_flat = local[:, shard_qkv + shard_fc1 : shard_qkv + shard_fc1 + shard_ov].reshape(-1)
    ov_cols = round_up(-(-ov_flat.shape[0] // rows), LANES)
    ov_part = jnp.pad(ov_flat, (0, rows * ov_cols - ov_flat.shape[0])).reshape(rows, ov_cols)
    qkv_part = jnp.concatenate(
        [
            lax.dynamic_slice_in_dim(qkv_rows, j * width + position * cols, cols, axis=1)
            for j in range(3)
        ]
        + [jnp.zeros((rows, pad_cols), bf16)],
        axis=1,
    )
    fc1_part = jnp.pad(
        lax.dynamic_slice_in_dim(fc1_rows, position * units, units, axis=1),
        ((0, 0), (0, pad_units)),
    )
    fc2_chunk = lax.ppermute(pack(w_fc2), both, to_quarter).reshape(-1)[:shard_fc2]
    fc2_part = jnp.pad(fc2_chunk.reshape(rows, units), ((0, 0), (0, pad_units)))
    weights = gather(jnp.concatenate([qkv_part, fc1_part, fc2_part, ov_part], axis=1), "img")
    end_qkv = 3 * cols + pad_cols
    end_fc1 = end_qkv + units + pad_units
    end_fc2 = end_fc1 + units + pad_units
    mat_qkv = weights[:, :end_qkv]
    mat_fc1 = weights[:, end_qkv:end_fc1]
    mat_fc2 = jnp.pad(
        weights[:, end_fc1 : end_fc1 + units].reshape(units, width), ((0, pad_units), (0, 0))
    )
    out_vec = weights[:, end_fc2:].reshape(img_count, -1)[:, : seq_count * shard_ov]
    cot_all = gather(cotangent[0], "seq")

    blocks_ov = out_vec.reshape(device_count, -1)
    mat_out = blocks_ov[:, :shard_out].reshape(width, width)
    vec = blocks_ov[:, shard_out : shard_out + shard_vec].reshape(-1).astype(f32)
    bias1, v_bias, gain1, q_bias, out_bias, gain2, bias2, fc2_bias = (
        vec[i * width : (i + 1) * width] for i in range(8)
    )
    fc1_bias = vec[8 * width : 8 * width + hidden]

    def my_cols(values):
        return lax.dynamic_slice_in_dim(values, position * cols, cols)

    fc1_bias_mine = jnp.pad(
        lax.dynamic_slice_in_dim(fc1_bias, position * units, units), (0, pad_units)
    )

    x = x_all16.astype(f32)
    normed1, _ = normalize(x)
    ln1 = (normed1 * gain1 + bias1).astype(bf16)
    qkv = jnp.dot(ln1, mat_qkv, preferred_element_type=f32)

    def by_head(values):
        return values.reshape(-1, heads, HEAD_DIM).transpose(1, 0, 2)

    def by_slot(values):
        return values.transpose(1, 0, 2).reshape(-1, cols)

    queries = by_head((qkv[:, :cols] + my_cols(q_bias)).astype(bf16))
    keys = by_head(qkv[:, cols : 2 * cols].astype(bf16))
    values = by_head((qkv[:, 2 * cols : 3 * cols] + my_cols(v_bias)).astype(bf16))
    scores = batched(queries, keys, 2, 2) * scale
    scores = jnp.where(key_valid[None, None, :], scores, -1e30)
    top = jnp.max(scores, axis=-1, keepdims=True)
    lse = top + jnp.log(jnp.sum(jnp.exp(scores - top), axis=-1, keepdims=True))
    probs = jnp.exp(scores - lse).astype(bf16)
    mixed_heads = batched(probs, values, 2, 1)
    mixed_mine = by_slot(mixed_heads).astype(bf16)
    mixed = lax.all_gather(mixed_mine, "seq", axis=0, tiled=True)
    mixed = (
        mixed.reshape(seq_count, -1, cols).transpose(1, 0, 2).reshape(-1, width)
    )
    resid = x + jnp.dot(mixed, mat_out, preferred_element_type=f32) + out_bias
    normed2, rstd2 = normalize(resid)
    ln2 = (normed2 * gain2 + bias2).astype(bf16)
    pre = jnp.dot(ln2, mat_fc1, preferred_element_type=f32) + fc1_bias_mine
    act_f, slope = gelu_parts(pre)
    act = act_f.astype(bf16)

    grad_y16 = jnp.where(key_valid[:, None], cot_all, jnp.zeros((), bf16))
    grad_pre = dot_t(grad_y16, mat_fc2) * slope
    grad_pre16 = grad_pre.astype(bf16)
    grad_ln2 = scatter_sum(dot_t(grad_pre16, mat_fc1).astype(bf16), "seq").astype(f32)
    grad_y = cotangent[0].astype(f32) * rowmask
    normed2_mine = mine(normed2)
    grad_resid = grad_y + norm_back(grad_ln2, normed2_mine, mine(rstd2), gain2)
    grad_resid16 = gather(grad_resid.astype(bf16), "seq")

    part_fc1 = weight_grad(ln2, grad_pre16)
    part_fc2 = pack_blocks(weight_grad(act, grad_y16)[:units].reshape(-1), img_count)
    out_terms = scatter_sum(
        jnp.dot(act, mat_fc2, preferred_element_type=f32).astype(bf16), "seq"
    ).astype(f32)
    output = ((mine(resid) + out_terms + fc2_bias) * rowmask).astype(bf16)

    out_mine = lax.dynamic_slice_in_dim(mat_out, position * cols, cols)
    gm = by_head(dot_t(grad_resid16, out_mine).astype(bf16))
    mixed_back = by_head(mixed_mine)
    delta = jnp.sum(gm.astype(f32) * mixed_back.astype(f32), axis=-1, keepdims=True)
    grad_values = by_slot(batched(probs, gm, 1, 1))
    dots = batched(gm, values, 2, 2)
    grad_scores = (jnp.exp(scores - lse) * (dots - delta) * scale).astype(bf16)
    grad_queries = by_slot(batched(grad_scores, keys, 2, 1))
    grad_keys = by_slot(batched(grad_scores, queries, 1, 1))
    grad_qkv16 = jnp.concatenate(
        [grad_queries.astype(bf16), grad_keys.astype(bf16), grad_values.astype(bf16)]
        + [jnp.zeros((seq_count * slot, pad_cols), bf16)],
        axis=1,
    )
    grad_ln1 = scatter_sum(dot_t(grad_qkv16, mat_qkv).astype(bf16), "seq").astype(f32)
    part_qkv = weight_grad(ln1, grad_qkv16)
    part_out = pack_blocks(weight_grad(mixed_mine, grad_resid16).reshape(-1), img_count)
    normed1_mine, rstd1_mine = normalize(tokens[0].astype(f32))
    input_grad = grad_resid + norm_back(grad_ln1, normed1_mine, rstd1_mine, gain1)

    def spread(part, full):
        return lax.dynamic_update_slice_in_dim(
            jnp.zeros((full,), f32), part, position * part.shape[0], 0
        )

    shard_front = 2 * width // device_count
    unused = shard_vec * device_count - 8 * width - hidden
    g_front = jnp.concatenate(
        [jnp.sum(grad_ln1, axis=0), spread(jnp.sum(grad_values, axis=0), width)]
    )
    g_rest = jnp.concatenate(
        [
            jnp.sum(grad_ln1 * normed1_mine, axis=0),
            spread(jnp.sum(grad_queries, axis=0), width),
            jnp.sum(grad_resid, axis=0),
            jnp.sum(grad_ln2 * normed2_mine, axis=0),
            jnp.sum(grad_ln2, axis=0),
            jnp.sum(grad_y, axis=0),
            spread(jnp.sum(grad_pre, axis=0)[:units], hidden),
            jnp.zeros((unused,), f32),
        ]
    )
    g_vec = jnp.concatenate(
        [g_front.reshape(device_count, -1), g_rest.reshape(device_count, -1)], axis=1
    )
    vec_pad = round_up(shard_vec, 4 * LANES)
    part_vec = jnp.pad(g_vec, ((0, 0), (0, vec_pad - shard_vec))).astype(bf16)

    parts = [
        part.reshape(img_count, -1, LANES)
        for part in (part_qkv, part_fc1, part_vec, part_fc2, part_out)
    ]
    sizes = [part.shape[1] for part in parts]
    summed = scatter_sum(jnp.concatenate(parts, axis=1).reshape(-1, LANES), "img")
    ends = [sum(sizes[: i + 1]) for i in range(5)]
    chunks = lax.ppermute(summed[ends[2] :], both, to_owner)
    grad_fc2 = chunks[: sizes[3]].reshape(-1)[:shard_fc2].astype(f32)
    grad_out = chunks[sizes[3] :].reshape(-1)[:shard_out].astype(f32)
    shared = gather(summed[: ends[2]], "seq").reshape(seq_count, ends[2], LANES)

    def own_block(packed, thirds, used, size):
        blocks = packed.reshape(seq_count, rows, -1)[:, :, : thirds * used]
        whole = blocks.reshape(seq_count, rows, thirds, used).transpose(1, 2, 0, 3)
        return lax.dynamic_slice_in_dim(whole.reshape(-1), position * size, size).astype(f32)

    grad_qkv = own_block(shared[:, : ends[0]], 3, cols, shard_qkv)
    grad_fc1 = own_block(shared[:, ends[0] : ends[1]], 1, units, shard_fc1)
    vec_sums = jnp.sum(shared[:, ends[1] :].astype(f32), axis=0).reshape(seq_count, vec_pad)
    vec_mine = lax.dynamic_slice_in_dim(vec_sums, position, 1).reshape(-1)
    return (
        output[None],
        input_grad[None],
        grad_qkv,
        grad_out,
        grad_fc1,
        grad_fc2,
        vec_mine[shard_front:shard_vec],
        vec_mine[:shard_front],
    )


def solution(mesh):
    return jax.shard_map(
        shards,
        mesh=mesh,
        in_specs=(
            P("img", "seq", None),
            P("img", None),
            P(("img", "seq")),
            P(("img", "seq")),
            P(("img", "seq")),
            P(("img", "seq")),
            P(("img", "seq")),
            P("img", "seq", None),
        ),
        out_specs=(
            P("img", "seq", None),
            P("img", "seq", None),
            P(("img", "seq")),
            P(("img", "seq")),
            P(("img", "seq")),
            P(("img", "seq")),
            P(("img", "seq")),
            P(("img", "seq")),
        ),
        check_vma=False,
    )
```
